256 devices in a mesh: wide: 32 (over x, z), narrow: 8 (over y, core).
Axes of the slice: x: 4, y: 4, z: 8, core: 2. Of those that a mesh axis runs over, the one named last changes fastest.
Arguments:
- tile_data: bfloat16 [81920, 128, 128], P(('wide', 'narrow')), may hold values from -0.119628906 to 0.119628906
- tile_user: int32 [81920], P(('wide', 'narrow')), may hold values from 0 to 63
- tile_item: int32 [81920], P(('wide', 'narrow')), may hold values from 0 to 31
- tile_word: int32 [81920], P(('wide', 'narrow')), may hold values from 0 to 4095
- tile_month: int32 [81920], P(('wide', 'narrow')), may hold values from 0 to 999
- tile_live: int32 [256], P(('wide', 'narrow')), may hold values from 160 to 320, as said below
- user_need: int32 [256, 64], P(('wide', 'narrow')), may hold values from 0 to 511, as said below
- item_need: int32 [256, 32], P(('wide', 'narrow')), may hold values from 0 to 511, as said below
- user_slot: int32 [512], replicated, may hold values from 0 to 511, as said below
- item_slot: int32 [512], replicated, may hold values from 0 to 511, as said below
- user_factor: bfloat16 [65536, 128], P('wide'), may hold values from -6 to 6
- word_factor: bfloat16 [4096, 128], replicated, may hold values from -6 to 6
- month_factor: bfloat16 [1000, 128], replicated, may hold values from -6 to 6
Outputs:
- item_rows: float32 [65536, 128], P(('wide', 'narrow'))
The draws below stay inside these ranges and needn't reach their ends.
Inputs may be any that keep to these rules, and one draw needn't show every extreme that they name: user_slot is a permutation; the owner of user block b is user_slot[b] // 16. item_slot is a permutation; the owner of item block b is item_slot[b] // 16. `user_need`: entries k * 2 to k * 2 + 1 of each row are distinct user blocks whose owner is k. `item_need`: entry k of each row is an item block whose owner is k. `tile_live`: some device has all its slots live.
All inputs are finite; a program needn't handle non-finite values.
Results may differ from the reference program's by a relative error of at most 0.0029.
Values may be sent and summed in bfloat16 or wider, within the bound.
A program may use at most 128 MiB of HBM per device.

```python
import jax
import jax.numpy as jnp
from jax import lax

R = 128
BS = 128
WORDS = 4096
MONTHS = 1000
TILES_DEV = 320
UB_OWN = 16
IB_OWN = 16
UPO = 2
IPO = 1
NDEV = 256
TILES = 81920
NUB = 512
NIB = 512
N_WIDE = 32


def choose_owned(key, per_owner, owned, inverse):
    scores = jax.random.randint(key, (NDEV, N_WIDE, owned), 0, 1 << 20) * owned
    scores = scores + jnp.arange(owned, dtype=jnp.int32)[None, None, :]
    picked = jnp.argsort(scores, axis=-1)[:, :, :per_owner].astype(jnp.int32)
    position = picked + (jnp.arange(N_WIDE, dtype=jnp.int32) * owned)[None, :, None]
    return inverse[position].reshape(NDEV, N_WIDE * per_owner).astype(jnp.int32)


def layout_tables(key):
    base = jax.random.fold_in(key, 9173)
    keys = jax.random.split(base, 8)
    user_slot = jax.random.permutation(keys[0], NUB).astype(jnp.int32)
    item_slot = jax.random.permutation(keys[1], NIB).astype(jnp.int32)
    user_inverse = jnp.argsort(user_slot).astype(jnp.int32)
    item_inverse = jnp.argsort(item_slot).astype(jnp.int32)
    user_need = choose_owned(keys[2], UPO, UB_OWN, user_inverse)
    item_need = choose_owned(keys[3], IPO, IB_OWN, item_inverse)
    tile_user = jax.random.randint(keys[4], (NDEV * TILES_DEV,), 0, N_WIDE * UPO).astype(jnp.int32)
    tile_item = jax.random.randint(keys[5], (NDEV * TILES_DEV,), 0, N_WIDE * IPO).astype(jnp.int32)
    tile_live = jax.random.randint(keys[6], (NDEV,), TILES_DEV // 2, TILES_DEV + 1).astype(jnp.int32)
    fullest = jax.random.randint(keys[7], (), 0, NDEV)
    tile_live = tile_live.at[fullest].set(TILES_DEV)
    return (user_slot, item_slot, user_need, item_need, tile_user, tile_item, tile_live)


def draw_user_slot(key, part):
    return layout_tables(key)[0]


def draw_item_slot(key, part):
    return layout_tables(key)[1]


def draw_user_need(key, part):
    return layout_tables(key)[2]


def draw_item_need(key, part):
    return layout_tables(key)[3]


def draw_tile_user(key, part):
    return layout_tables(key)[4]


def draw_tile_item(key, part):
    return layout_tables(key)[5]


def draw_tile_live(key, part):
    return layout_tables(key)[6]


def place_ends(values, rng, least, largest):
    dims = values.shape
    spot = [jax.random.randint(jax.random.fold_in(rng, axis), (), 0, dims[axis]) for axis in range(len(dims))]
    values = values.at[tuple(spot)].set(least)
    longest = dims.index(max(dims))
    spot[longest] = (spot[longest] + 1) % dims[longest]
    return values.at[tuple(spot)].set(largest)


def block_levels(stream_key, dims, cuts, least, largest):
    gain, own = 1.0, jax.random.fold_in(stream_key, 6)
    for dim, parts in cuts:
        heights = jnp.exp(jax.random.uniform(jax.random.fold_in(own, dim), (parts,), jnp.float32, least / len(cuts), largest / len(cuts)))
        gain = gain * jnp.repeat(heights, dims[dim] // parts).reshape([-1 if axis == dim else 1 for axis in range(len(dims))])
    return gain


def gaussian(key, extent, width, reach, cuts=(), held_as=jnp.bfloat16):
    gain = block_levels(key, extent, cuts, -0.22, 0.18) if cuts else 1.0
    result = jax.random.normal(key, extent, jnp.float32) * width * gain
    return jnp.minimum(jnp.maximum(result, -reach), reach).astype(held_as)


def setup_inputs(seed: int = 0) -> dict:
    splits = jax.random.split(jax.random.key(seed), 14)
    return {
        "tile_data": gaussian(splits[0], (TILES, BS, BS), 0.02, 0.119628906, ((0, 256),)),
        "tile_user": draw_tile_user(jax.random.fold_in(splits[13], 71), 0),
        "tile_item": draw_tile_item(jax.random.fold_in(splits[13], 71), 0),
        "tile_word": place_ends(jax.random.randint(splits[3], (TILES,), 0, WORDS), jax.random.fold_in(splits[3], 1), 0, WORDS - 1).astype(jnp.int32),
        "tile_month": place_ends(jax.random.randint(splits[4], (TILES,), 0, MONTHS), jax.random.fold_in(splits[4], 1), 0, MONTHS - 1).astype(jnp.int32),
        "tile_live": draw_tile_live(jax.random.fold_in(splits[13], 71), 0),
        "user_need": draw_user_need(jax.random.fold_in(splits[13], 71), 0),
        "item_need": draw_item_need(jax.random.fold_in(splits[13], 71), 0),
        "user_slot": draw_user_slot(jax.random.fold_in(splits[13], 71), 0),
        "item_slot": draw_item_slot(jax.random.fold_in(splits[13], 71), 0),
        "user_factor": gaussian(splits[10], (NUB * BS, R), 1.0, 6.0, ((0, 32),)),
        "word_factor": gaussian(splits[11], (WORDS, R), 1.0, 6.0),
        "month_factor": gaussian(splits[12], (MONTHS, R), 1.0, 6.0),
    }


def reference(tile_data, tile_user, tile_item, tile_word, tile_month, tile_live, user_need, item_need, user_slot, item_slot, user_factor, word_factor, month_factor):
    user_block = jnp.take_along_axis(user_need, tile_user.reshape(NDEV, TILES_DEV), axis=1)
    user_stored = user_slot[user_block].astype(jnp.int32)
    item_block = jnp.take_along_axis(item_need, tile_item.reshape(NDEV, TILES_DEV), axis=1)
    item_stored = item_slot[item_block].astype(jnp.int32)
    live_mask = (lax.iota(jnp.int32, TILES_DEV)[None, :] < tile_live[:, None]).astype(jnp.float32)
    factor_blocks = user_factor.reshape(NUB, BS, R)
    word_month = word_factor[tile_word].astype(jnp.float32) * month_factor[tile_month].astype(jnp.float32)
    word_month = word_month.reshape(NDEV, TILES_DEV, R)

    def one_device(total, packed):
        data, stored, target, factor_scale, mask = packed
        scaled = (factor_blocks[stored].astype(jnp.float32) * factor_scale[:, None, :]).astype(jnp.bfloat16)
        contrib = jnp.einsum("tab,tar->tbr", data.astype(jnp.float32), scaled.astype(jnp.float32))
        contrib = contrib * mask[:, None, None]
        return total.at[target].add(contrib), None

    start = jnp.zeros((NIB, BS, R), jnp.float32)
    total, _ = lax.scan(one_device, start, (tile_data.reshape(NDEV, TILES_DEV, BS, BS), user_stored, item_stored, word_month, live_mask))
    return total.reshape(NIB * BS, R)
```

```python
import functools

import jax
import jax.numpy as jnp
from jax import lax
from jax.experimental import pallas as pl
from jax.experimental.pallas import tpu as pltpu
from jax.sharding import PartitionSpec as P

MESH = pl.DeviceIdType.MESH
ANY = pl.BlockSpec(memory_space=pl.ANY)
VMEM = pl.BlockSpec(memory_space=pltpu.VMEM)
SMEM = pl.BlockSpec(memory_space=pltpu.SMEM)
DMA = pltpu.SemaphoreType.DMA


def place(zs):
    wide, n = lax.axis_index("wide"), lax.axis_index("narrow")
    return wide // zs, lax.rem(wide, zs), n


def fetch_kernel(
    peers, ns, upo, needs, factor, fetched, table, held, packed, landed, table_s,
    local_sem, table_send, table_recv, line_send, line_recv, pack_send, pack_recv,
):
    zs = qs = ns
    x, z, n = place(zs)
    me = x * ns + n

    def plane(p):
        return (p // ns * zs + z, lax.rem(p, ns))

    def line(d):
        return (x * zs + lax.rem(z + d, zs), n)

    barrier = pltpu.get_barrier_semaphore()

    @pl.loop(1, peers)
    def _(r):
        pl.semaphore_signal(barrier, inc=1, device_id=plane(lax.rem(me + r, peers)), device_id_type=MESH)

    @pl.loop(1, zs)
    def _(d):
        pl.semaphore_signal(barrier, inc=1, device_id=line(d), device_id_type=MESH)

    pl.semaphore_wait(barrier, peers - 1 + zs - 1)

    def table_copy(p, slot, r):
        return pltpu.make_async_remote_copy(
            src_ref=needs, dst_ref=table.at[slot], send_sem=table_send.at[r], recv_sem=table_recv.at[slot],
            device_id=plane(p), device_id_type=MESH,
        )

    def line_copy(d, chunk):
        return pltpu.make_async_remote_copy(
            src_ref=factor.at[:, chunk], dst_ref=held.at[d], send_sem=line_send.at[d], recv_sem=line_recv.at[d],
            device_id=line(zs - d), device_id_type=MESH,
        )

    def pack_copy(p, slot, r):
        return pltpu.make_async_remote_copy(
            src_ref=packed.at[r], dst_ref=landed.at[slot], send_sem=pack_send.at[r], recv_sem=pack_recv.at[slot],
            device_id=plane(p), device_id_type=MESH,
        )

    @pl.loop(1, peers)
    def _(r):
        table_copy(lax.rem(me + r, peers), me, r).start()

    own = pltpu.make_async_copy(factor.at[:, lax.rem(ns - n, qs)], held.at[0], local_sem)
    own.start()

    @pl.loop(1, zs)
    def _(d):
        line_copy(d, lax.rem(d + ns - n, qs)).start()

    table[me] = needs[...]

    @pl.loop(1, peers)
    def _(r):
        p = lax.rem(me + r, peers)
        table_copy(p, p, r).wait_recv()

    own.wait()
    to_scalar = pltpu.make_async_copy(table, table_s, local_sem)
    to_scalar.start()
    to_scalar.wait()

    @pl.loop(1, zs)
    def _(d):
        line_copy(d, 0).wait_recv()

    def pack(p, target, at):
        for d in range(zs):
            owner = x * zs + lax.rem(z + d, zs)
            for i in range(upo):
                target[at, d * upo + i] = held[d, table_s[p, 0, owner * upo + i]]

    @pl.loop(1, peers)
    def _(r):
        p = lax.rem(me + r, peers)
        pack(p, packed, r)
        pack_copy(p, me, r).start()

    pack(me, landed, me)

    def unpack(p):
        px, pn = p // ns, lax.rem(p, ns)
        for d in range(zs):
            owner = px * zs + lax.rem(z + d, zs)
            q = lax.rem(d + ns - pn, qs)
            for i in range(upo):
                fetched[owner * upo + i, q] = landed[p, d * upo + i]

    unpack(me)

    @pl.loop(1, peers)
    def _(r):
        p = lax.rem(me + peers - r, peers)
        pack_copy(p, p, r).wait_recv()
        unpack(p)

    @pl.loop(1, peers)
    def _(r):
        table_copy(me, me, r).wait_send()
        pack_copy(me, me, r).wait_send()

    @pl.loop(1, zs)
    def _(d):
        line_copy(d, 0).wait_send()


def tile_kernel(
    ns, unroll, parts, tile_user, tile_item, live, place_s, data, fetched, scale, packed,
    buffer, total, data_sem,
):
    tiles, touched = buffer.shape[0], total.shape[0] - 1
    zs = qs = ns
    z = place_s[0]
    per = tiles // parts
    rows = packed.shape[2]

    def data_copy(c):
        span = pl.ds(c * per, per)
        return pltpu.make_async_copy(data.at[span], buffer.at[span], data_sem.at[c])

    for c in range(parts):
        data_copy(c).start()
    total[...] = jnp.zeros_like(total)

    def step(s, carry):
        terms = []
        for k in range(unroll):
            t = s * unroll + k
            block = fetched[tile_user[t]].astype(jnp.float32)
            scaled = (block * scale[pl.ds(t, 1), :]).astype(jnp.bfloat16)
            term = lax.dot_general(
                buffer[t], scaled, (((0,), (0,)), ((), ())), preferred_element_type=jnp.float32
            )
            terms.append((jnp.where(t < live[0], tile_item[t], touched), term))
        for item, term in terms:
            total[item] += term
        return carry

    for c in range(parts):
        data_copy(c).wait()
        lax.fori_loop(c * per // unroll, (c + 1) * per // unroll, step, 0)

    @pl.loop(0, touched)
    def _(k):
        kx, d = k // zs, lax.rem(lax.rem(k, zs) + zs - z, zs)
        for q in range(qs):
            pn = lax.rem(d + ns - q, ns)
            packed[kx * ns + pn, q] = total[k, q * rows : (q + 1) * rows, :].astype(packed.dtype)


def reduce_kernel(
    peers, ns, owned, previous, final, packed, out, arrived, sums, leaving, landed,
    local_sem, plane_send, plane_recv, last_send, last_recv,
):
    zs = qs = ns
    x, z, n = place(zs)
    me = x * ns + n
    each = owned // ns

    def plane(p):
        return (p // ns * zs + z, lax.rem(p, ns))

    def sheet(d, m):
        return (x * zs + lax.rem(z + d, zs), lax.rem(n + m, ns))

    barrier = pltpu.get_barrier_semaphore()

    @pl.loop(1, peers)
    def _(r):
        pl.semaphore_signal(barrier, inc=1, device_id=plane(lax.rem(me + r, peers)), device_id_type=MESH)

    @pl.loop(1, zs * ns)
    def _(r):
        pl.semaphore_signal(barrier, inc=1, device_id=sheet(r // ns, lax.rem(r, ns)), device_id_type=MESH)

    pl.semaphore_wait(barrier, peers - 1 + zs * ns - 1)

    def plane_copy(p, slot, r):
        return pltpu.make_async_remote_copy(
            src_ref=packed.at[p], dst_ref=arrived.at[slot], send_sem=plane_send.at[r], recv_sem=plane_recv.at[slot],
            device_id=plane(p), device_id_type=MESH,
        )

    @pl.loop(1, peers)
    def _(r):
        plane_copy(lax.rem(me + r, peers), me, r).start()

    own = pltpu.make_async_copy(packed.at[me], arrived.at[me], local_sem)
    own.start()
    sums[0] = jnp.zeros_like(sums[0])
    own.wait()

    @pl.loop(1, peers)
    def _(r):
        p = lax.rem(me + peers - r, peers)
        plane_copy(p, p, r).wait_recv()

    @pl.loop(0, peers)
    def _(i):
        for q in range(qs):
            sums[i + 1, q] = sums[previous[i * qs + q], q] + arrived[i, q].astype(jnp.float32)

    def last_copy(d, m, source, q):
        return pltpu.make_async_remote_copy(
            src_ref=leaving.at[d, lax.rem(n + m, ns)],
            dst_ref=landed.at[source, q],
            send_sem=last_send.at[d * ns + m],
            recv_sem=last_recv.at[source * qs + q],
            device_id=sheet(d, m),
            device_id_type=MESH,
        )

    def leave(d):
        q = lax.rem(d + ns - n, qs)
        for j in range(owned):
            leaving[d, j // each, j % each] = sums[final[q * owned + j], q].astype(leaving.dtype)
        return q

    @pl.loop(1, zs)
    def _(d):
        q = leave(d)

        @pl.loop(0, ns)
        def _(m):
            last_copy(d, m, z, q).start()

    q0 = leave(0)

    @pl.loop(1, ns)
    def _(m):
        last_copy(0, m, z, q0).start()

    landed[z, q0] = leaving[0, n]

    @pl.loop(0, qs)
    def _(q):
        @pl.when(q != q0)
        def _():
            last_copy(1, 0, z, q).wait_recv()

    @pl.loop(1, zs)
    def _(d):
        @pl.loop(0, qs)
        def _(q):
            last_copy(1, 0, lax.rem(z + d, zs), q).wait_recv()

    @pl.loop(0, qs)
    def _(q):
        for s in range(each):
            value = landed[0, q, s].astype(jnp.float32)
            for source in range(1, zs):
                value += landed[source, q, s].astype(jnp.float32)
            out[s, q] = value

    @pl.loop(1, peers)
    def _(r):
        plane_copy(me, me, r).wait_send()

    @pl.loop(1, zs * ns)
    def _(r):
        last_copy(r // ns, lax.rem(r, ns), z, 0).wait_send()


def shards(
    tile_data,
    tile_user,
    tile_item,
    tile_word,
    tile_month,
    tile_live,
    user_need,
    item_need,
    user_slot,
    item_slot,
    user_factor,
    word_factor,
    month_factor,
):
    wide, ns = lax.axis_size("wide"), lax.axis_size("narrow")
    zs = qs = ns
    peers = wide // zs * ns
    tiles, side = tile_data.shape[:2]
    rank = user_factor.shape[1]
    rows = side // qs
    owned_u, owned_i = user_slot.shape[0] // wide, item_slot.shape[0] // wide
    used, touched = user_need.shape[1], item_need.shape[1]
    upo = used // wide
    lanes = -(-(used + touched) // 128) * 128
    x, z, n = place(zs)

    names = jnp.concatenate([user_need[0], item_need[0] + user_slot.shape[0]])
    slots = jnp.concatenate([user_slot % owned_u, item_slot % owned_i])
    hit = names[:, None] == lax.iota(jnp.int32, slots.shape[0])[None, :]
    needs = jnp.sum(jnp.where(hit, slots[None, :], 0), axis=1)
    needs = jnp.pad(needs, (0, lanes - used - touched)).reshape(1, lanes)

    fetched, table = pl.pallas_call(
        functools.partial(fetch_kernel, peers, ns, upo),
        out_shape=(
            jax.ShapeDtypeStruct((used, qs, rows, rank), jnp.bfloat16),
            jax.ShapeDtypeStruct((peers, 1, lanes), jnp.int32),
        ),
        in_specs=[VMEM, ANY],
        out_specs=(VMEM, VMEM),
        scratch_shapes=[
            pltpu.VMEM((zs, owned_u, rows, rank), jnp.bfloat16),
            pltpu.VMEM((peers, zs * upo, rows, rank), jnp.bfloat16),
            pltpu.VMEM((peers, zs * upo, rows, rank), jnp.bfloat16),
            pltpu.SMEM((peers, 1, lanes), jnp.int32),
            DMA,
            DMA((peers,)),
            DMA((peers,)),
            DMA((zs,)),
            DMA((zs,)),
            DMA((peers,)),
            DMA((peers,)),
        ],
        compiler_params=pltpu.CompilerParams(
            collective_id=0, has_side_effects=True, vmem_limit_bytes=20 << 20
        ),
        name="fetch",
    )(needs, user_factor.reshape(owned_u, qs, rows, rank))

    word_month = word_factor[tile_word].astype(jnp.float32) * month_factor[tile_month].astype(jnp.float32)

    packed = pl.pallas_call(
        functools.partial(tile_kernel, ns, 16, tiles // 32 * 2),
        out_shape=jax.ShapeDtypeStruct((peers, qs, rows, rank), jnp.bfloat16),
        grid_spec=pltpu.PrefetchScalarGridSpec(
            num_scalar_prefetch=4,
            grid=(),
            in_specs=[ANY, VMEM, VMEM],
            out_specs=VMEM,
            scratch_shapes=[
                pltpu.VMEM((tiles, side, side), jnp.bfloat16),
                pltpu.VMEM((touched + 1, side, rank), jnp.float32),
                DMA((tiles // 32 * 2,)),
            ],
        ),
        compiler_params=pltpu.CompilerParams(vmem_limit_bytes=40 << 20),
        name="tiles",
    )(
        tile_user, tile_item, tile_live, z.reshape(1),
        tile_data, fetched.reshape(used, side, rank), word_month,
    )

    columns = used + x * zs + (z + (n + lax.iota(jnp.int32, qs)) % zs) % zs
    pick = columns[None, :, None] == lax.iota(jnp.int32, lanes)[None, None, :]
    targets = jnp.sum(jnp.where(pick, table, 0), axis=2)
    order = lax.iota(jnp.int32, peers)
    same = (targets[:, None, :] == targets[None, :, :]) & (order[None, :, None] < order[:, None, None])
    previous = jnp.max(jnp.where(same, order[None, :, None] + 1, 0), axis=1)
    mine = targets[:, :, None] == lax.iota(jnp.int32, owned_i)[None, None, :]
    final = jnp.max(jnp.where(mine, order[:, None, None] + 1, 0), axis=0)

    each = owned_i // ns
    out = pl.pallas_call(
        functools.partial(reduce_kernel, peers, ns, owned_i),
        out_shape=jax.ShapeDtypeStruct((each, qs, rows, rank), jnp.float32),
        in_specs=[SMEM, SMEM, ANY],
        out_specs=VMEM,
        scratch_shapes=[
            pltpu.VMEM((peers, qs, rows, rank), jnp.bfloat16),
            pltpu.VMEM((peers + 1, qs, rows, rank), jnp.float32),
            pltpu.VMEM((zs, ns, each, rows, rank), jnp.bfloat16),
            pltpu.VMEM((zs, qs, each, rows, rank), jnp.bfloat16),
            DMA,
            DMA((peers,)),
            DMA((peers,)),
            DMA((zs * ns,)),
            DMA((zs * qs,)),
        ],
        compiler_params=pltpu.CompilerParams(
            collective_id=1, has_side_effects=True, vmem_limit_bytes=20 << 20
        ),
        name="reduce",
    )(previous.reshape(-1), final.reshape(-1), packed)
    return out.reshape(-1, rank)


def solution(mesh):
    return jax.shard_map(
        shards,
        mesh=mesh,
        in_specs=(
            P(("wide", "narrow"), None, None),
            P(("wide", "narrow")),
            P(("wide", "narrow")),
            P(("wide", "narrow")),
            P(("wide", "narrow")),
            P(("wide", "narrow")),
            P(("wide", "narrow"), None),
            P(("wide", "narrow"), None),
            P(),
            P(),
            P("wide", None),
            P(),
            P(),
        ),
        out_specs=P(("wide", "narrow"), None),
        check_vma=False,
    )
```

```python
import functools

import jax
import jax.numpy as jnp
from jax import lax
from jax.experimental import pallas as pl
from jax.experimental.pallas import tpu as pltpu
from jax.sharding import PartitionSpec as P

MESH = pl.DeviceIdType.MESH
HBM = pl.BlockSpec(memory_space=pltpu.HBM)
VMEM = pl.BlockSpec(memory_space=pltpu.VMEM)
SMEM = pl.BlockSpec(memory_space=pltpu.SMEM)
DMA = pltpu.SemaphoreType.DMA
F32, BF16, I32 = jnp.float32, jnp.bfloat16, jnp.int32


def place(zs):
    wide, n = lax.axis_index("wide"), lax.axis_index("narrow")
    return wide // zs, lax.rem(wide, zs), n


def line_stages(zs):
    order = [0]
    for d in range(1, zs // 2 + 1):
        order += [d] if 2 * d == zs else [d, zs - d]
    if zs < 8:
        return order, [(0, 1), (1, zs)]
    return order, [(0, 1), (1, 3), (3, 5), (5, zs)]


def kernel(
    peers, ns, upo, unroll, parts,
    user_need, item_need, user_slot, item_slot, tile_user, tile_word, tile_month, tile_before, tile_last,
    data, factor, words, months,
    out,
    row_s, table_s, before_s, last_s,
    needs, table, flat, index_v, last_v, held, packed, landed, fetched, words_in, months_in, words_f, months_f,
    scale, buffer, chain, sending, arrived, sums, leaving, final,
    local_sem, held_sem, words_sem, months_sem, data_sem,
    table_send, table_recv, line_send, line_recv, pack_send, pack_recv,
    plane_send, plane_recv, last_send, last_recv,
):
    zs = qs = ns
    x, z, n = place(zs)
    me = x * ns + n
    tiles = buffer.shape[0]
    rows = held[0].shape[1]
    owned_u, owned_i = held[0].shape[0], leaving.shape[1] * leaving.shape[2]
    used, touched = user_need.shape[1], item_need.shape[1]
    each = owned_i // ns
    order, stages = line_stages(zs)

    def plane(p):
        return (p // ns * zs + z, lax.rem(p, ns))

    def sheet(d, m):
        return (x * zs + lax.rem(z + d, zs), lax.rem(n + m, ns))

    def remote(source, target, send, recv, device):
        return pltpu.make_async_remote_copy(
            src_ref=source, dst_ref=target, send_sem=send, recv_sem=recv, device_id=device, device_id_type=MESH
        )

    barrier = pltpu.get_barrier_semaphore()

    @pl.loop(1, peers)
    def _(r):
        pl.semaphore_signal(barrier, inc=1, device_id=plane(lax.rem(me + r, peers)), device_id_type=MESH)

    @pl.loop(ns, zs * ns)
    def _(r):
        pl.semaphore_signal(barrier, inc=1, device_id=sheet(r // ns, lax.rem(r, ns)), device_id_type=MESH)

    words_copy = pltpu.make_async_copy(words, words_in, words_sem)
    months_copy = pltpu.make_async_copy(months, months_in, months_sem)
    words_copy.start()
    months_copy.start()
    held_copy = pltpu.make_async_copy(factor.at[:, lax.rem(ns - n, qs)], held[0], held_sem)
    held_copy.start()

    for k in range(row_s.shape[1] - used - touched):
        row_s[0, used + touched + k] = 0

    @pl.loop(0, used)
    def _(k):
        row_s[0, k] = lax.rem(user_slot[user_need[0, k]], owned_u)

    @pl.loop(0, touched)
    def _(k):
        row_s[0, used + k] = lax.rem(item_slot[item_need[0, k]], owned_i)

    row_copy = pltpu.make_async_copy(row_s, needs, local_sem)
    row_copy.start()
    row_copy.wait()

    pl.semaphore_wait(barrier, peers - 1 + (zs - 1) * ns)

    def table_copy(p, slot, r):
        return remote(needs, table.at[slot], table_send.at[r], table_recv.at[slot], plane(p))

    def line_copy(d, chunk):
        return remote(factor.at[:, chunk], held[d], line_send.at[d], line_recv.at[d], sheet(zs - d, 0))

    def pack_copy(stage, p, slot, r):
        a, b = stages[stage]
        span = pl.ds(a * upo, (b - a) * upo)
        return remote(
            packed.at[r, span], landed.at[slot, span],
            pack_send.at[stage, r], pack_recv.at[stage, slot], plane(p),
        )

    @pl.loop(1, peers)
    def _(r):
        table_copy(lax.rem(me + r, peers), me, r).start()

    for d in order[1:]:
        line_copy(d, lax.rem(d + ns - n, qs)).start()

    per = tiles // parts

    def data_copy(c):
        span = pl.ds(c * per, per)
        return pltpu.make_async_copy(data.at[span], buffer.at[span], data_sem.at[c])

    @pl.loop(0, parts)
    def _(c):
        data_copy(c).start()

    table[me] = needs[...]

    words_copy.wait()
    months_copy.wait()
    words_f[...] = words_in[...].astype(F32)
    months_f[...] = months_in[...].astype(F32)

    @pl.loop(0, tiles // 8)
    def _(s):
        for k in range(8):
            t = s * 8 + k
            scale[pl.ds(t, 1), :] = words_f[pl.ds(tile_word[t], 1), :] * months_f[pl.ds(tile_month[t], 1), :]

    @pl.loop(1, peers)
    def _(r):
        p = lax.rem(me + r, peers)
        table_copy(p, p, r).wait_recv()

    to_scalar = pltpu.make_async_copy(table, table_s, local_sem)
    to_scalar.start()
    to_scalar.wait()

    def pack(stage, p, target, at):
        for pos in range(*stages[stage]):
            d = order[pos]
            owner = x * zs + lax.rem(z + d, zs)
            for i in range(upo):
                target[at, pos * upo + i] = held[d][table_s[p, 0, owner * upo + i]]

    for stage, (a, b) in enumerate(stages):
        if stage == 0:
            held_copy.wait()
        for pos in range(max(a, 1), b):
            line_copy(order[pos], 0).wait_recv()

        @pl.loop(1, peers)
        def _(r):
            p = lax.rem(me + r, peers)
            pack(stage, p, packed, r)
            pack_copy(stage, p, me, r).start()

        pack(stage, me, landed, me)

    @pl.loop(0, peers)
    def _(p):
        flat[pl.ds(p, 1), :] = table[p]

    lanes = flat.shape[1]
    lane = lax.broadcasted_iota(I32, (peers, lanes), 1)
    sub = lax.broadcasted_iota(I32, (peers, lanes), 0)
    slots_lane = lax.broadcasted_iota(I32, (owned_i, lanes), 1)
    slots_sub = lax.broadcasted_iota(I32, (owned_i, lanes), 0)
    entries = flat[...]
    befores, lasts = jnp.zeros((peers, lanes), I32), jnp.zeros((owned_i, lanes), I32)
    for q in range(qs):
        column = used + x * zs + lax.rem(z + lax.rem(n + q, zs), zs)
        down = jnp.sum(jnp.where(lane == column, entries, 0), axis=1, keepdims=True)
        down = jnp.broadcast_to(down, (peers, lanes))
        along = jnp.sum(jnp.where(lane == sub, down, 0), axis=0, keepdims=True)
        same = (down == jnp.broadcast_to(along, (peers, lanes))) & (lane < sub)
        before = jnp.max(jnp.where(same, lane + 1, 0), axis=1, keepdims=True)
        befores = jnp.where(lane == q, jnp.broadcast_to(before, (peers, lanes)), befores)
        mine = (jnp.broadcast_to(along, (owned_i, lanes)) == slots_sub) & (slots_lane < peers)
        last = jnp.max(jnp.where(mine, slots_lane + 1, 0), axis=1, keepdims=True)
        lasts = jnp.where(slots_lane == q, jnp.broadcast_to(last, (owned_i, lanes)), lasts)
    index_v[...] = befores
    last_v[...] = lasts
    index_copy = pltpu.make_async_copy(index_v, before_s, local_sem)
    index_copy.start()
    index_copy.wait()
    final_copy = pltpu.make_async_copy(last_v, last_s, local_sem)
    final_copy.start()
    final_copy.wait()

    chain[0] = jnp.zeros_like(chain[0])
    sums[0] = jnp.zeros_like(sums[0])

    def unpack(stage, p):
        px, pn = p // ns, lax.rem(p, ns)
        for pos in range(*stages[stage]):
            d = order[pos]
            owner = px * zs + lax.rem(z + d, zs)
            q = lax.rem(d + ns - pn, qs)
            at = pl.ds(pl.multiple_of(q * rows, rows), rows)
            for i in range(upo):
                fetched[owner * upo + i, at, :] = landed[p, pos * upo + i]

    for stage in range(len(stages)):
        unpack(stage, me)

        @pl.loop(1, peers)
        def _(r):
            p = lax.rem(me + peers - r, peers)
            pack_copy(stage, p, p, r).wait_recv()
            unpack(stage, p)

    @pl.loop(0, parts)
    def _(c):
        data_copy(c).wait()

    @pl.loop(0, tiles // unroll)
    def _(s):
        terms = []
        for k in range(unroll):
            t = s * unroll + k
            scaled = (fetched[tile_user[t]].astype(F32) * scale[pl.ds(t, 1), :]).astype(BF16)
            terms.append(
                lax.dot_general(buffer[t], scaled, (((0,), (0,)), ((), ())), preferred_element_type=F32)
            )
        for k, term in enumerate(terms):
            t = s * unroll + k
            chain[t + 1] = chain[tile_before[t]] + term

    steps = plane_send.shape[0]
    group = qs // steps

    def plane_copy(step, p, slot, r):
        return remote(
            sending.at[step, p], arrived.at[step, slot], plane_send.at[step, r], plane_recv.at[step, slot], plane(p)
        )

    def load(step, p, target, at):
        px, pn = p // ns, lax.rem(p, ns)
        for j in range(group):
            q = step * group + j
            k = px * zs + lax.rem(z + lax.rem(pn + q, zs), zs)
            target[step, at, j] = chain[tile_last[k], q * rows : (q + 1) * rows, :].astype(BF16)

    for step in range(steps):
        @pl.loop(1, peers)
        def _(r):
            p = lax.rem(me + r, peers)
            load(step, p, sending, p)
            plane_copy(step, p, me, r).start()

        load(step, me, arrived, me)

    def last_copy(q, d, m, source):
        return remote(
            leaving.at[q, lax.rem(n + m, ns)], final.at[source, q],
            last_send.at[q * ns + m], last_recv.at[source * qs + q], sheet(d, m),
        )

    for step in range(steps):
        @pl.loop(1, peers)
        def _(r):
            p = lax.rem(me + peers - r, peers)
            plane_copy(step, p, p, r).wait_recv()

        @pl.loop(0, peers)
        def _(i):
            for j in range(group):
                q = step * group + j
                sums[i + 1, q] = sums[before_s[i, q], q] + arrived[step, i, j].astype(F32)

        for j in range(group):
            q = step * group + j
            d = lax.rem(n + q, zs)
            for slot in range(owned_i):
                leaving[q, slot // each, slot % each] = sums[last_s[slot, q], q].astype(BF16)

            @pl.when(d == 0)
            def _():
                final[z, q] = leaving[q, n]

                @pl.loop(1, ns)
                def _(m):
                    last_copy(q, d, m, z).start()

            @pl.when(d != 0)
            def _():
                @pl.loop(0, ns)
                def _(m):
                    last_copy(q, d, m, z).start()

    for q in range(qs):
        @pl.when(lax.rem(n + q, zs) != 0)
        def _():
            last_copy(q, 1, 0, z).wait_recv()

        @pl.loop(1, zs)
        def _(d):
            last_copy(q, 1, 0, lax.rem(z + d, zs)).wait_recv()

        for s in range(each):
            value = final[0, q, s].astype(F32)
            for source in range(1, zs):
                value += final[source, q, s].astype(F32)
            out[s, q] = value

    @pl.loop(1, peers)
    def _(r):
        table_copy(me, me, r).wait_send()
        for stage in range(len(stages)):
            pack_copy(stage, me, me, r).wait_send()
        for step in range(steps):
            plane_copy(step, me, me, r).wait_send()

    for d in order[1:]:
        line_copy(d, 0).wait_send()

    for q in range(qs):
        @pl.when(lax.rem(n + q, zs) != 0)
        def _():
            last_copy(q, 1, 0, z).wait_send()

        @pl.loop(1, ns)
        def _(m):
            last_copy(q, 1, m, z).wait_send()


def shards(
    tile_data,
    tile_user,
    tile_item,
    tile_word,
    tile_month,
    tile_live,
    user_need,
    item_need,
    user_slot,
    item_slot,
    user_factor,
    word_factor,
    month_factor,
):
    wide, ns = lax.axis_size("wide"), lax.axis_size("narrow")
    zs = qs = ns
    peers = wide // zs * ns
    tiles, side = tile_data.shape[:2]
    rank = user_factor.shape[1]
    rows = side // qs
    owned_u, owned_i = user_slot.shape[0] // wide, item_slot.shape[0] // wide
    used, touched = user_need.shape[1], item_need.shape[1]
    upo, each = used // wide, owned_i // ns
    lanes = -(-(used + touched) // 128) * 128
    stages = len(line_stages(zs)[1])
    steps = min(4, qs)
    parts = min(16, tiles // 16)

    index = lax.iota(I32, tiles)
    same = (tile_item[:, None] == tile_item[None, :]) & (index[None, :] < index[:, None])
    tile_before = jnp.max(jnp.where(same, index[None, :] + 1, 0), axis=1)
    mine = (tile_item[None, :] == lax.iota(I32, touched)[:, None]) & (index < tile_live[0])[None, :]
    tile_last = jnp.max(jnp.where(mine, index[None, :] + 1, 0), axis=1)

    out = pl.pallas_call(
        functools.partial(kernel, peers, ns, upo, 16, parts),
        out_shape=jax.ShapeDtypeStruct((each, qs, rows, rank), F32),
        in_specs=[SMEM] * 9 + [HBM] * 4,
        out_specs=VMEM,
        scratch_shapes=[
            pltpu.SMEM((1, lanes), I32),
            pltpu.SMEM((peers, 1, lanes), I32),
            pltpu.SMEM((peers, lanes), I32),
            pltpu.SMEM((owned_i, lanes), I32),
            pltpu.VMEM((1, lanes), I32),
            pltpu.VMEM((peers, 1, lanes), I32),
            pltpu.VMEM((peers, lanes), I32),
            pltpu.VMEM((peers, lanes), I32),
            pltpu.VMEM((owned_i, lanes), I32),
            [pltpu.VMEM((owned_u, rows, rank), BF16)] * zs,
            pltpu.VMEM((peers, zs * upo, rows, rank), BF16),
            pltpu.VMEM((peers, zs * upo, rows, rank), BF16),
            pltpu.VMEM((used, side, rank), BF16),
            pltpu.VMEM(word_factor.shape, BF16),
            pltpu.VMEM(month_factor.shape, BF16),
            pltpu.VMEM(word_factor.shape, F32),
            pltpu.VMEM(month_factor.shape, F32),
            pltpu.VMEM((tiles, rank), F32),
            pltpu.VMEM((tiles, side, side), BF16),
            pltpu.VMEM((tiles + 1, side, rank), F32),
            pltpu.VMEM((steps, peers, qs // steps, rows, rank), BF16),
            pltpu.VMEM((steps, peers, qs // steps, rows, rank), BF16),
            pltpu.VMEM((peers + 1, qs, rows, rank), F32),
            pltpu.VMEM((qs, ns, each, rows, rank), BF16),
            pltpu.VMEM((zs, qs, each, rows, rank), BF16),
            DMA,
            DMA,
            DMA,
            DMA,
            DMA((parts,)),
            DMA((peers,)),
            DMA((peers,)),
            DMA((zs,)),
            DMA((zs,)),
            DMA((stages, peers)),
            DMA((stages, peers)),
            DMA((steps, peers)),
            DMA((steps, peers)),
            DMA((qs * ns,)),
            DMA((zs * qs,)),
        ],
        compiler_params=pltpu.CompilerParams(
            collective_id=0, has_side_effects=True, vmem_limit_bytes=58 << 20
        ),
        name="mttkrp",
    )(
        user_need, item_need, user_slot, item_slot, tile_user, tile_word, tile_month, tile_before, tile_last,
        tile_data, user_factor.reshape(owned_u, qs, rows, rank), word_factor, month_factor,
    )
    return out.reshape(-1, rank)


def solution(mesh):
    return jax.shard_map(
        shards,
        mesh=mesh,
        in_specs=(
            P(("wide", "narrow"), None, None),
            P(("wide", "narrow")),
            P(("wide", "narrow")),
            P(("wide", "narrow")),
            P(("wide", "narrow")),
            P(("wide", "narrow")),
            P(("wide", "narrow"), None),
            P(("wide", "narrow"), None),
            P(),
            P(),
            P("wide", None),
            P(),
            P(),
        ),
        out_specs=P(("wide", "narrow"), None),
        check_vma=False,
    )
```

```python
import functools

import jax
import jax.numpy as jnp
from jax import lax
from jax.experimental import pallas as pl
from jax.experimental.pallas import tpu as pltpu
from jax.sharding import PartitionSpec as P

MESH = pl.DeviceIdType.MESH
HBM = pl.BlockSpec(memory_space=pltpu.HBM)
DMA = pltpu.SemaphoreType.DMA
F32, BF16, I32 = jnp.float32, jnp.bfloat16, jnp.int32


def place(zs):
    wide, n = lax.axis_index("wide"), lax.axis_index("narrow")
    return wide // zs, lax.rem(wide, zs), n


def line_stages(zs):
    order = [0]
    for d in range(1, zs // 2 + 1):
        order += [d] if 2 * d == zs else [d, zs - d]
    if zs < 8:
        return order, [(0, 1), (1, zs)]
    return order, [(0, 1), (1, 3), (3, 5), (5, zs)]


def kernel(
    peers, ns, upo, unroll,
    user_need_h, item_need_h, user_slot_h, item_slot_h, tile_user_h, tile_word_h, tile_month_h, tile_live_h,
    tile_item_h, data, factor, words, months,
    final,
    user_need, item_need, user_slot, item_slot, tile_user, tile_word, tile_month, tile_live,
    row_s, table_s, before_s, last_s, tile_before, tile_last,
    items_v, tile_before_v, tile_last_v, needs, table, flat, index_v, last_v, held, packed, landed, fetched, words_in, months_in, words_f, months_f,
    scale, buffer, chain, sending, arrived, sums, leaving,
    small_sem, items_sem, stay_sem, local_sem, held_sem, words_sem, months_sem, data_sem,
    table_send, table_recv, line_send, line_recv, pack_send, pack_recv,
    plane_send, plane_recv, last_send, last_recv,
):
    zs = qs = ns
    x, z, n = place(zs)
    me = x * ns + n
    tiles = buffer.shape[0]
    rows = held[0].shape[1]
    owned_u, owned_i = held[0].shape[0], leaving.shape[1] * leaving.shape[2]
    used, touched = user_need.shape[1], item_need.shape[1]
    each = owned_i // ns
    order, stages = line_stages(zs)

    def plane(p):
        return (p // ns * zs + z, lax.rem(p, ns))

    def sheet(d, m):
        return (x * zs + lax.rem(z + d, zs), lax.rem(n + m, ns))

    def remote(source, target, send, recv, device):
        return pltpu.make_async_remote_copy(
            src_ref=source, dst_ref=target, send_sem=send, recv_sem=recv, device_id=device, device_id_type=MESH
        )

    barrier = pltpu.get_barrier_semaphore()

    @pl.loop(1, peers)
    def _(r):
        pl.semaphore_signal(barrier, inc=1, device_id=plane(lax.rem(me + r, peers)), device_id_type=MESH)

    @pl.loop(ns, zs * ns)
    def _(r):
        pl.semaphore_signal(barrier, inc=1, device_id=sheet(r // ns, lax.rem(r, ns)), device_id_type=MESH)

    small = [
        pltpu.make_async_copy(source, target, small_sem.at[i])
        for i, (source, target) in enumerate((
            (user_need_h, user_need), (item_need_h, item_need), (user_slot_h, user_slot), (item_slot_h, item_slot),
            (tile_user_h, tile_user), (tile_word_h, tile_word), (tile_month_h, tile_month), (tile_live_h, tile_live),
        ))
    ]
    for copy in small:
        copy.start()
    items_copy = pltpu.make_async_copy(tile_item_h, items_v, items_sem)
    items_copy.start()
    words_copy = pltpu.make_async_copy(words, words_in, words_sem)
    months_copy = pltpu.make_async_copy(months, months_in, months_sem)
    words_copy.start()
    months_copy.start()
    held_copy = pltpu.make_async_copy(factor.at[:, lax.rem(ns - n, qs)], held[0], held_sem)
    held_copy.start()

    for copy in small:
        copy.wait()

    for k in range(row_s.shape[1] - used - touched):
        row_s[0, used + touched + k] = 0

    @pl.loop(0, used)
    def _(k):
        row_s[0, k] = lax.rem(user_slot[user_need[0, k]], owned_u)

    @pl.loop(0, touched)
    def _(k):
        row_s[0, used + k] = lax.rem(item_slot[item_need[0, k]], owned_i)

    row_copy = pltpu.make_async_copy(row_s, needs, local_sem)
    row_copy.start()
    row_copy.wait()

    pl.semaphore_wait(barrier, peers - 1 + (zs - 1) * ns)

    def table_copy(p, slot, r):
        return remote(needs, table.at[slot], table_send, table_recv, plane(p))

    def line_copy(d, chunk):
        return remote(factor.at[:, chunk], held[d], line_send, line_recv.at[d], sheet(zs - d, 0))

    def pack_copy(stage, p, slot, r):
        a, b = stages[stage]
        span = pl.ds(a * upo, (b - a) * upo)
        return remote(
            packed.at[r, span], landed.at[slot, span],
            pack_send.at[stage], pack_recv.at[stage], plane(p),
        )

    @pl.loop(1, peers)
    def _(r):
        table_copy(lax.rem(me + r, peers), me, r).start()

    for d in order[1:]:
        line_copy(d, lax.rem(d + ns - n, qs)).start()

    data_copy = pltpu.make_async_copy(data, buffer, data_sem)
    data_copy.start()
    table[me] = needs[...]

    words_copy.wait()
    months_copy.wait()
    words_f[...] = words_in[...].astype(F32)
    months_f[...] = months_in[...].astype(F32)

    @pl.loop(0, tiles // 8)
    def _(s):
        for k in range(8):
            t = s * 8 + k
            scale[pl.ds(t, 1), :] = words_f[pl.ds(tile_word[t], 1), :] * months_f[pl.ds(tile_month[t], 1), :]

    items_copy.wait()
    wide = 128
    pieces = -(-tiles // wide)
    lane = lax.broadcasted_iota(I32, (wide, wide), 1)
    sub = lax.broadcasted_iota(I32, (wide, wide), 0)
    down, along = [], []
    for c in range(pieces):
        size = min(wide, tiles - c * wide)
        line = jnp.broadcast_to(items_v[c * wide : c * wide + size].reshape(1, size), (wide, size))
        if size < wide:
            line = jnp.concatenate([line, jnp.full((wide, wide - size), -1, I32)], axis=1)
        column = jnp.sum(jnp.where(lane == sub, line, 0), axis=1, keepdims=True)
        along.append(line)
        down.append(jnp.broadcast_to(column, (wide, wide)))
    latest = jnp.zeros((1, wide), I32)
    for c in range(pieces):
        number = sub + (c * wide + 1)
        mine = (down[c] == lane) & (number <= tile_live[0])
        latest = jnp.maximum(latest, jnp.max(jnp.where(mine, number, 0), axis=0, keepdims=True))
        before = jnp.zeros((1, wide), I32)
        for b in range(c + 1):
            number = sub + (b * wide + 1)
            same = (down[b] == along[c]) & (number < lane + (c * wide + 1))
            before = jnp.maximum(before, jnp.max(jnp.where(same, number, 0), axis=0, keepdims=True))
        tile_before_v[:, c * wide : (c + 1) * wide] = before
    tile_last_v[...] = latest
    before_copy = pltpu.make_async_copy(tile_before_v, tile_before, local_sem)
    before_copy.start()
    before_copy.wait()
    latest_copy = pltpu.make_async_copy(tile_last_v, tile_last, local_sem)
    latest_copy.start()
    latest_copy.wait()

    others = pl.ds(0, peers - 1)
    table_all = remote(table.at[others], table.at[others], table_send, table_recv, plane(me))
    table_all.wait_recv()

    to_scalar = pltpu.make_async_copy(table, table_s, local_sem)
    to_scalar.start()
    to_scalar.wait()

    def pack(stage, p, target, at):
        for pos in range(*stages[stage]):
            d = order[pos]
            owner = x * zs + lax.rem(z + d, zs)
            for i in range(upo):
                target[at, pos * upo + i] = held[d][table_s[p, 0, owner * upo + i]]

    for stage, (a, b) in enumerate(stages):
        if stage == 0:
            held_copy.wait()
        for pos in range(max(a, 1), b):
            line_copy(order[pos], 0).wait_recv()

        @pl.loop(1, peers)
        def _(r):
            p = lax.rem(me + r, peers)
            pack(stage, p, packed, r)
            pack_copy(stage, p, me, r).start()

        pack(stage, me, landed, me)

    @pl.loop(0, peers)
    def _(p):
        flat[pl.ds(p, 1), :] = table[p]

    lanes = flat.shape[1]
    lane = lax.broadcasted_iota(I32, (peers, lanes), 1)
    sub = lax.broadcasted_iota(I32, (peers, lanes), 0)
    slots_lane = lax.broadcasted_iota(I32, (owned_i, lanes), 1)
    slots_sub = lax.broadcasted_iota(I32, (owned_i, lanes), 0)
    entries = flat[...]
    befores, lasts = jnp.zeros((peers, lanes), I32), jnp.zeros((owned_i, lanes), I32)
    for q in range(qs):
        column = used + x * zs + lax.rem(z + lax.rem(n + q, zs), zs)
        down = jnp.sum(jnp.where(lane == column, entries, 0), axis=1, keepdims=True)
        down = jnp.broadcast_to(down, (peers, lanes))
        along = jnp.sum(jnp.where(lane == sub, down, 0), axis=0, keepdims=True)
        same = (down == jnp.broadcast_to(along, (peers, lanes))) & (lane < sub)
        before = jnp.max(jnp.where(same, lane + 1, 0), axis=1, keepdims=True)
        befores = jnp.where(lane == q, jnp.broadcast_to(before, (peers, lanes)), befores)
        mine = (jnp.broadcast_to(along, (owned_i, lanes)) == slots_sub) & (slots_lane < peers)
        last = jnp.max(jnp.where(mine, slots_lane + 1, 0), axis=1, keepdims=True)
        lasts = jnp.where(slots_lane == q, jnp.broadcast_to(last, (owned_i, lanes)), lasts)
    index_v[...] = befores
    last_v[...] = lasts
    index_copy = pltpu.make_async_copy(index_v, before_s, local_sem)
    index_copy.start()
    index_copy.wait()
    final_copy = pltpu.make_async_copy(last_v, last_s, local_sem)
    final_copy.start()
    final_copy.wait()

    chain[0] = jnp.zeros_like(chain[0])
    sums[0] = jnp.zeros_like(sums[0])

    def unpack(stage, p):
        px, pn = p // ns, lax.rem(p, ns)
        for pos in range(*stages[stage]):
            d = order[pos]
            owner = px * zs + lax.rem(z + d, zs)
            q = lax.rem(d + ns - pn, qs)
            at = pl.ds(pl.multiple_of(q * rows, rows), rows)
            for i in range(upo):
                fetched[owner * upo + i, at, :] = landed[p, pos * upo + i]

    def pack_all(stage):
        a, b = stages[stage]
        span = pl.ds(a * upo, (b - a) * upo)
        return remote(
            packed.at[others, span], landed.at[others, span], pack_send.at[stage], pack_recv.at[stage], plane(me)
        )

    for stage in range(len(stages)):
        pack_all(stage).wait_recv()

        @pl.loop(0, peers)
        def _(p):
            unpack(stage, p)

    data_copy.wait()

    @pl.loop(0, tiles // unroll)
    def _(s):
        terms = []
        for k in range(unroll):
            t = s * unroll + k
            scaled = (fetched[tile_user[t]].astype(F32) * scale[pl.ds(t, 1), :]).astype(BF16)
            terms.append(
                lax.dot_general(buffer[t], scaled, (((0,), (0,)), ((), ())), preferred_element_type=F32)
            )
        for k, term in enumerate(terms):
            t = s * unroll + k
            chain[t + 1] = chain[tile_before[0, t]] + term

    steps = plane_send.shape[0]
    group = qs // steps

    def plane_copy(step, p, slot, r):
        return remote(
            sending.at[step, p], arrived.at[step, slot], plane_send.at[step], plane_recv.at[step], plane(p)
        )

    def load(step, p, target, at):
        px, pn = p // ns, lax.rem(p, ns)
        for j in range(group):
            q = step * group + j
            k = px * zs + lax.rem(z + lax.rem(pn + q, zs), zs)
            target[step, at, j] = chain[tile_last[0, k], q * rows : (q + 1) * rows, :].astype(BF16)

    for step in range(steps):
        @pl.loop(1, peers)
        def _(r):
            p = lax.rem(me + r, peers)
            load(step, p, sending, p)
            plane_copy(step, p, me, r).start()

        load(step, me, arrived, me)

    def last_copy(far, q, d, m):
        return remote(
            leaving.at[q, lax.rem(n + m, ns)], final.at[z, :, q], last_send.at[far], last_recv.at[far], sheet(d, m)
        )

    def plane_all(step):
        return remote(
            sending.at[step, others], arrived.at[step, others], plane_send.at[step], plane_recv.at[step], plane(me)
        )

    def stay_copy(q):
        return pltpu.make_async_copy(leaving.at[q, n], final.at[z, :, q], stay_sem)

    for step in range(steps):
        plane_all(step).wait_recv()

        @pl.loop(0, peers)
        def _(i):
            for j in range(group):
                q = step * group + j
                sums[i + 1, q] = sums[before_s[i, q], q] + arrived[step, i, j].astype(F32)

        for j in range(group):
            q = step * group + j
            d = lax.rem(n + q, zs)
            for slot in range(owned_i):
                leaving[q, slot // each, slot % each] = sums[last_s[slot, q], q].astype(BF16)

            @pl.when(d == 0)
            def _():
                stay_copy(q).start()

                @pl.loop(1, ns)
                def _(m):
                    last_copy(0, q, d, m).start()

            @pl.when(d != 0)
            def _():
                @pl.loop(0, ns)
                def _(m):
                    last_copy(1, q, d, m).start()

    most = pl.ds(0, zs - 1)
    near_all = remote(leaving.at[0, most], final.at[z, :, most], last_send.at[0], last_recv.at[0], sheet(0, 0))
    far_all = remote(leaving.at[most], final.at[most], last_send.at[1], last_recv.at[1], sheet(0, 0))
    near_all.wait_recv()
    far_all.wait_recv()
    stay_copy(0).wait()

    table_all.wait_send()
    lines = remote(factor.at[:, most], factor.at[:, most], line_send, line_recv.at[0], sheet(0, 0))
    lines.wait_send()
    for stage in range(len(stages)):
        pack_all(stage).wait_send()
    for step in range(steps):
        plane_all(step).wait_send()
    near_all.wait_send()
    far_all.wait_send()


def shards(
    tile_data,
    tile_user,
    tile_item,
    tile_word,
    tile_month,
    tile_live,
    user_need,
    item_need,
    user_slot,
    item_slot,
    user_factor,
    word_factor,
    month_factor,
):
    wide, ns = lax.axis_size("wide"), lax.axis_size("narrow")
    zs = qs = ns
    peers = wide // zs * ns
    tiles, side = tile_data.shape[:2]
    rank = user_factor.shape[1]
    rows = side // qs
    owned_u, owned_i = user_slot.shape[0] // wide, item_slot.shape[0] // wide
    used, touched = user_need.shape[1], item_need.shape[1]
    upo, each = used // wide, owned_i // ns
    lanes = -(-(used + touched) // 128) * 128
    stages = len(line_stages(zs)[1])
    steps = min(4, qs)

    final = pl.pallas_call(
        functools.partial(kernel, peers, ns, upo, 16),
        out_shape=jax.ShapeDtypeStruct((zs, each, qs, rows, rank), BF16),
        in_specs=[HBM] * 13,
        out_specs=HBM,
        scratch_shapes=[
            pltpu.SMEM(user_need.shape, I32),
            pltpu.SMEM(item_need.shape, I32),
            pltpu.SMEM(user_slot.shape, I32),
            pltpu.SMEM(item_slot.shape, I32),
            pltpu.SMEM((tiles,), I32),
            pltpu.SMEM((tiles,), I32),
            pltpu.SMEM((tiles,), I32),
            pltpu.SMEM((1,), I32),
            pltpu.SMEM((1, lanes), I32),
            pltpu.SMEM((peers, 1, lanes), I32),
            pltpu.SMEM((peers, lanes), I32),
            pltpu.SMEM((owned_i, lanes), I32),
            pltpu.SMEM((1, -(-tiles // 128) * 128), I32),
            pltpu.SMEM((1, 128), I32),
            pltpu.VMEM((tiles,), I32),
            pltpu.VMEM((1, -(-tiles // 128) * 128), I32),
            pltpu.VMEM((1, 128), I32),
            pltpu.VMEM((1, lanes), I32),
            pltpu.VMEM((peers, 1, lanes), I32),
            pltpu.VMEM((peers, lanes), I32),
            pltpu.VMEM((peers, lanes), I32),
            pltpu.VMEM((owned_i, lanes), I32),
            [pltpu.VMEM((owned_u, rows, rank), BF16)] * zs,
            pltpu.VMEM((peers, zs * upo, rows, rank), BF16),
            pltpu.VMEM((peers, zs * upo, rows, rank), BF16),
            pltpu.VMEM((used, side, rank), BF16),
            pltpu.VMEM(word_factor.shape, BF16),
            pltpu.VMEM(month_factor.shape, BF16),
            pltpu.VMEM(word_factor.shape, F32),
            pltpu.VMEM(month_factor.shape, F32),
            pltpu.VMEM((tiles, rank), F32),
            pltpu.VMEM((tiles, side, side), BF16),
            pltpu.VMEM((tiles + 1, side, rank), F32),
            pltpu.VMEM((steps, peers, qs // steps, rows, rank), BF16),
            pltpu.VMEM((steps, peers, qs // steps, rows, rank), BF16),
            pltpu.VMEM((peers + 1, qs, rows, rank), F32),
            pltpu.VMEM((qs, ns, each, rows, rank), BF16),
            DMA((8,)),
            DMA,
            DMA,
            DMA,
            DMA,
            DMA,
            DMA,
            DMA,
            DMA,
            DMA,
            DMA,
            DMA((zs,)),
            DMA((stages,)),
            DMA((stages,)),
            DMA((steps,)),
            DMA((steps,)),
            DMA((2,)),
            DMA((2,)),
        ],
        compiler_params=pltpu.CompilerParams(
            collective_id=0, has_side_effects=True, vmem_limit_bytes=58 << 20
        ),
        name="mttkrp",
    )(
        user_need, item_need, user_slot, item_slot, tile_user, tile_word, tile_month, tile_live,
        tile_item, tile_data, user_factor.reshape(owned_u, qs, rows, rank), word_factor, month_factor,
    )
    return jnp.sum(final.astype(F32), axis=0).reshape(-1, rank)


def solution(mesh):
    return jax.shard_map(
        shards,
        mesh=mesh,
        in_specs=(
            P(("wide", "narrow"), None, None),
            P(("wide", "narrow")),
            P(("wide", "narrow")),
            P(("wide", "narrow")),
            P(("wide", "narrow")),
            P(("wide", "narrow")),
            P(("wide", "narrow"), None),
            P(("wide", "narrow"), None),
            P(),
            P(),
            P("wide", None),
            P(),
            P(),
        ),
        out_specs=P(("wide", "narrow"), None),
        check_vma=False,
    )
```

```python
import functools

import jax
import jax.numpy as jnp
from jax import lax
from jax.experimental import pallas as pl
from jax.experimental.pallas import tpu as pltpu
from jax.sharding import PartitionSpec as P

MESH = pl.DeviceIdType.MESH
HBM = pl.BlockSpec(memory_space=pltpu.HBM)
DMA = pltpu.SemaphoreType.DMA
F32, BF16, I32 = jnp.float32, jnp.bfloat16, jnp.int32


def place(zs):
    wide, n = lax.axis_index("wide"), lax.axis_index("narrow")
    return wide // zs, lax.rem(wide, zs), n


def line_order(zs):
    order = [0]
    for d in range(1, zs // 2 + 1):
        order += [d] if 2 * d == zs else [d, zs - d]
    return order


def kernel(
    peers, ns, upo, unroll,
    user_need_h, item_need_h, user_slot_h, item_slot_h, tile_user_h, tile_word_h, tile_month_h, tile_live_h,
    tile_item_h, data, factor, words, months,
    final,
    user_need, item_need, user_slot, item_slot, tile_user, tile_word, tile_month, tile_live,
    row_s, table_s, before_s, last_s, tile_before, tile_last,
    items_v, tile_before_v, tile_last_v, needs, table, flat, index_v, last_v, held, packed, landed, fetched, words_in, months_in, words_f, months_f,
    scale, buffer, chain, sending, arrived, sums, leaving,
    small_sem, items_sem, stay_sem, local_sem, held_sem, words_sem, months_sem, data_sem,
    table_send, table_recv, line_send, line_recv, pack_send, pack_recv,
    plane_send, plane_recv, last_send, last_recv,
):
    zs = qs = ns
    x, z, n = place(zs)
    me = x * ns + n
    tiles = buffer.shape[0]
    rows = held[0].shape[1]
    owned_u, owned_i = held[0].shape[0], leaving.shape[1] * leaving.shape[2]
    used, touched = user_need.shape[1], item_need.shape[1]
    each = owned_i // ns
    order = line_order(zs)
    stages = [(pos, pos + 1) for pos in range(zs)]

    def plane(p):
        return (p // ns * zs + z, lax.rem(p, ns))

    def sheet(d, m):
        return (x * zs + lax.rem(z + d, zs), lax.rem(n + m, ns))

    def remote(source, target, send, recv, device):
        return pltpu.make_async_remote_copy(
            src_ref=source, dst_ref=target, send_sem=send, recv_sem=recv, device_id=device, device_id_type=MESH
        )

    barrier = pltpu.get_barrier_semaphore()

    @pl.loop(1, peers)
    def _(r):
        pl.semaphore_signal(barrier, inc=1, device_id=plane(lax.rem(me + r, peers)), device_id_type=MESH)

    @pl.loop(ns, zs * ns)
    def _(r):
        pl.semaphore_signal(barrier, inc=1, device_id=sheet(r // ns, lax.rem(r, ns)), device_id_type=MESH)

    small = [
        pltpu.make_async_copy(source, target, small_sem.at[i])
        for i, (source, target) in enumerate((
            (user_need_h, user_need), (item_need_h, item_need), (user_slot_h, user_slot), (item_slot_h, item_slot),
            (tile_user_h, tile_user), (tile_word_h, tile_word), (tile_month_h, tile_month), (tile_live_h, tile_live),
        ))
    ]
    for copy in small:
        copy.start()
    items_copy = pltpu.make_async_copy(tile_item_h, items_v, items_sem)
    items_copy.start()
    words_copy = pltpu.make_async_copy(words, words_in, words_sem)
    months_copy = pltpu.make_async_copy(months, months_in, months_sem)
    words_copy.start()
    months_copy.start()
    held_copy = pltpu.make_async_copy(factor.at[:, lax.rem(ns - n, qs)], held[0], held_sem)
    held_copy.start()

    for copy in small:
        copy.wait()

    for k in range(row_s.shape[1] - used - touched):
        row_s[0, used + touched + k] = 0

    @pl.loop(0, used)
    def _(k):
        row_s[0, k] = lax.rem(user_slot[user_need[0, k]], owned_u)

    @pl.loop(0, touched)
    def _(k):
        row_s[0, used + k] = lax.rem(item_slot[item_need[0, k]], owned_i)

    row_copy = pltpu.make_async_copy(row_s, needs, local_sem)
    row_copy.start()
    row_copy.wait()

    pl.semaphore_wait(barrier, peers - 1 + (zs - 1) * ns)

    def table_copy(p, slot, r):
        return remote(needs, table.at[slot], table_send, table_recv, plane(p))

    def line_copy(d, chunk):
        return remote(factor.at[:, chunk], held[d], line_send, line_recv.at[d], sheet(zs - d, 0))

    def pack_copy(stage, p, slot, r):
        a, b = stages[stage]
        span = pl.ds(a * upo, (b - a) * upo)
        return remote(
            packed.at[r, span], landed.at[slot, span],
            pack_send.at[stage], pack_recv.at[stage], plane(p),
        )

    @pl.loop(1, peers)
    def _(r):
        table_copy(lax.rem(me + r, peers), me, r).start()

    for d in order[1:]:
        line_copy(d, lax.rem(d + ns - n, qs)).start()

    data_copy = pltpu.make_async_copy(data, buffer, data_sem)
    data_copy.start()
    table[me] = needs[...]

    words_copy.wait()
    months_copy.wait()
    words_f[...] = words_in[...].astype(F32)
    months_f[...] = months_in[...].astype(F32)

    @pl.loop(0, tiles // 8)
    def _(s):
        for k in range(8):
            t = s * 8 + k
            scale[pl.ds(t, 1), :] = words_f[pl.ds(tile_word[t], 1), :] * months_f[pl.ds(tile_month[t], 1), :]

    items_copy.wait()
    wide = 128
    pieces = -(-tiles // wide)
    lane = lax.broadcasted_iota(I32, (wide, wide), 1)
    sub = lax.broadcasted_iota(I32, (wide, wide), 0)

    def count(mask, axis):
        return jnp.sum(jnp.where(mask, 1, 0), axis=axis, keepdims=True)

    def spread(value):
        return jnp.broadcast_to(value, (wide, wide))

    down, along = [], []
    for c in range(pieces):
        size = min(wide, tiles - c * wide)
        line = jnp.broadcast_to(items_v[c * wide : c * wide + size].reshape(1, size), (wide, size))
        if size < wide:
            line = jnp.concatenate([line, jnp.full((wide, wide - size), touched + 1, I32)], axis=1)
        alive = lane + c * wide < tile_live[0]
        line = jnp.where(alive, line, jnp.maximum(line, touched))
        along.append(line)
        down.append(spread(jnp.sum(jnp.where(lane == sub, line, 0), axis=1, keepdims=True)))
    reach, present = jnp.zeros((1, wide), I32), jnp.zeros((1, wide), I32)
    codes = [jnp.zeros((1, wide), I32) for _ in range(pieces)]
    for c in range(pieces):
        reach += count(down[c] <= lane, 0)
        present += count(down[c] == lane, 0)
        rank, repeats = jnp.zeros((wide, 1), I32), jnp.zeros((wide, 1), I32)
        for b in range(pieces):
            earlier = lane + b * wide < sub + c * wide
            same = (along[b] == down[c]) & earlier
            rank += count((along[b] < down[c]) | same, 1)
            repeats += count(same, 1)
        code = (sub + c * wide) * 2 + spread(jnp.minimum(repeats, 1))
        for b in range(pieces):
            codes[b] += jnp.sum(jnp.where(spread(rank) == lane + b * wide, code, 0), axis=0, keepdims=True)
    for c in range(pieces):
        tile_before_v[:, c * wide : (c + 1) * wide] = codes[c]
    tile_last_v[...] = jnp.where(present > 0, reach, 0)
    before_copy = pltpu.make_async_copy(tile_before_v, tile_before, local_sem)
    before_copy.start()
    before_copy.wait()
    latest_copy = pltpu.make_async_copy(tile_last_v, tile_last, local_sem)
    latest_copy.start()
    latest_copy.wait()

    others = pl.ds(0, peers - 1)
    table_all = remote(table.at[others], table.at[others], table_send, table_recv, plane(me))
    table_all.wait_recv()

    to_scalar = pltpu.make_async_copy(table, table_s, local_sem)
    to_scalar.start()
    to_scalar.wait()

    def pack(stage, p, target, at):
        for pos in range(*stages[stage]):
            d = order[pos]
            owner = x * zs + lax.rem(z + d, zs)
            for i in range(upo):
                target[at, pos * upo + i] = held[d][table_s[p, 0, owner * upo + i]]

    for stage, (a, b) in enumerate(stages):
        if stage == 0:
            held_copy.wait()
        for pos in range(max(a, 1), b):
            line_copy(order[pos], 0).wait_recv()

        @pl.loop(1, peers)
        def _(r):
            p = lax.rem(me + r, peers)
            pack(stage, p, packed, r)
            pack_copy(stage, p, me, r).start()

        pack(stage, me, landed, me)

    @pl.loop(0, peers)
    def _(p):
        flat[pl.ds(p, 1), :] = table[p]

    lanes = flat.shape[1]
    lane = lax.broadcasted_iota(I32, (peers, lanes), 1)
    sub = lax.broadcasted_iota(I32, (peers, lanes), 0)
    slots_lane = lax.broadcasted_iota(I32, (owned_i, lanes), 1)
    slots_sub = lax.broadcasted_iota(I32, (owned_i, lanes), 0)
    entries = flat[...]
    befores, lasts = jnp.zeros((peers, lanes), I32), jnp.zeros((owned_i, lanes), I32)
    for q in range(qs):
        column = used + x * zs + lax.rem(z + lax.rem(n + q, zs), zs)
        down = jnp.sum(jnp.where(lane == column, entries, 0), axis=1, keepdims=True)
        down = jnp.broadcast_to(down, (peers, lanes))
        along = jnp.sum(jnp.where(lane == sub, down, 0), axis=0, keepdims=True)
        along = jnp.broadcast_to(along, (peers, lanes))
        same = (down == along) & (sub < lane)
        rank = jnp.broadcast_to(count((down < along) | same, 0), (peers, lanes))
        code = 2 * lane + jnp.broadcast_to(jnp.minimum(count(same, 0), 1), (peers, lanes))
        before = jnp.sum(jnp.where((rank == sub) & (lane < peers), code, 0), axis=1, keepdims=True)
        befores = jnp.where(lane == q, jnp.broadcast_to(before, (peers, lanes)), befores)
        inside = slots_lane < peers
        target = jnp.broadcast_to(along[:1], (owned_i, lanes))
        reach = count((target <= slots_sub) & inside, 1)
        last = jnp.where(count((target == slots_sub) & inside, 1) > 0, reach, 0)
        lasts = jnp.where(slots_lane == q, jnp.broadcast_to(last, (owned_i, lanes)), lasts)
    index_v[...] = befores
    last_v[...] = lasts
    index_copy = pltpu.make_async_copy(index_v, before_s, local_sem)
    index_copy.start()
    index_copy.wait()
    final_copy = pltpu.make_async_copy(last_v, last_s, local_sem)
    final_copy.start()
    final_copy.wait()

    chain[0] = jnp.zeros_like(chain[0])
    sums[0] = jnp.zeros_like(sums[0])

    def unpack(stage, p):
        px, pn = p // ns, lax.rem(p, ns)
        for pos in range(*stages[stage]):
            d = order[pos]
            owner = px * zs + lax.rem(z + d, zs)
            q = lax.rem(d + ns - pn, qs)
            at = pl.ds(pl.multiple_of(q * rows, rows), rows)
            for i in range(upo):
                fetched[owner * upo + i, at, :] = landed[p, pos * upo + i]

    def pack_all(stage):
        a, b = stages[stage]
        span = pl.ds(a * upo, (b - a) * upo)
        return remote(
            packed.at[others, span], landed.at[others, span], pack_send.at[stage], pack_recv.at[stage], plane(me)
        )

    for stage in range(len(stages)):
        pack_all(stage).wait_recv()

        @pl.loop(0, peers)
        def _(p):
            unpack(stage, p)

    data_copy.wait()

    def step_tiles(s, total):
        terms = []
        for k in range(unroll):
            code = tile_before[0, s * unroll + k]
            t = code // 2
            scaled = (fetched[tile_user[t]].astype(F32) * scale[pl.ds(t, 1), :]).astype(BF16)
            term = lax.dot_general(buffer[t], scaled, (((0,), (0,)), ((), ())), preferred_element_type=F32)
            terms.append((lax.rem(code, 2).astype(F32), term))
        for k, (keep, term) in enumerate(terms):
            total = total * keep + term
            chain[s * unroll + k + 1] = total
        return total

    lax.fori_loop(0, tiles // unroll, step_tiles, jnp.zeros(chain.shape[1:], F32))

    steps = plane_send.shape[0]
    group = qs // steps

    def plane_copy(step, p, slot, r):
        return remote(
            sending.at[step, p], arrived[step].at[slot], plane_send.at[step], plane_recv.at[step], plane(p)
        )

    def load(step, p, target, at):
        px, pn = p // ns, lax.rem(p, ns)
        for j in range(group):
            q = step * group + j
            k = px * zs + lax.rem(z + lax.rem(pn + q, zs), zs)
            target[at, j] = chain[tile_last[0, k], q * rows : (q + 1) * rows, :].astype(BF16)

    for step in range(steps):
        @pl.loop(1, peers)
        def _(r):
            p = lax.rem(me + r, peers)
            load(step, p, sending.at[step], p)
            plane_copy(step, p, me, r).start()

        load(step, me, arrived[step], me)

    def last_copy(far, q, d, m):
        return remote(
            leaving.at[q, lax.rem(n + m, ns)], final.at[z, :, q], last_send.at[far], last_recv.at[far], sheet(d, m)
        )

    def plane_all(step):
        return remote(
            sending.at[step, others], arrived[step].at[others], plane_send.at[step], plane_recv.at[step], plane(me)
        )

    def stay_copy(q):
        return pltpu.make_async_copy(leaving.at[q, n], final.at[z, :, q], stay_sem)

    for step in range(steps):
        plane_all(step).wait_recv()

        for j in range(group):
            q = step * group + j

            def add(i, total):
                code = before_s[i, q]
                total = total * lax.rem(code, 2).astype(F32) + arrived[step][code // 2, j].astype(F32)
                sums[i + 1, q] = total
                return total

            lax.fori_loop(0, peers, add, jnp.zeros(sums.shape[2:], F32), unroll=4)

        for j in range(group):
            q = step * group + j
            d = lax.rem(n + q, zs)
            for slot in range(owned_i):
                leaving[q, slot // each, slot % each] = sums[last_s[slot, q], q].astype(BF16)

            @pl.when(d == 0)
            def _():
                stay_copy(q).start()

                @pl.loop(1, ns)
                def _(m):
                    last_copy(0, q, d, m).start()

            @pl.when(d != 0)
            def _():
                @pl.loop(0, ns)
                def _(m):
                    last_copy(1, q, d, m).start()

    most = pl.ds(0, zs - 1)
    near_all = remote(leaving.at[0, most], final.at[z, :, most], last_send.at[0], last_recv.at[0], sheet(0, 0))
    far_all = remote(leaving.at[most], final.at[most], last_send.at[1], last_recv.at[1], sheet(0, 0))
    near_all.wait_recv()
    far_all.wait_recv()
    stay_copy(0).wait()

    table_all.wait_send()
    lines = remote(factor.at[:, most], factor.at[:, most], line_send, line_recv.at[0], sheet(0, 0))
    lines.wait_send()
    for stage in range(len(stages)):
        pack_all(stage).wait_send()
    for step in range(steps):
        plane_all(step).wait_send()
    near_all.wait_send()
    far_all.wait_send()


def shards(
    tile_data,
    tile_user,
    tile_item,
    tile_word,
    tile_month,
    tile_live,
    user_need,
    item_need,
    user_slot,
    item_slot,
    user_factor,
    word_factor,
    month_factor,
):
    wide, ns = lax.axis_size("wide"), lax.axis_size("narrow")
    zs = qs = ns
    peers = wide // zs * ns
    tiles, side = tile_data.shape[:2]
    rank = user_factor.shape[1]
    rows = side // qs
    owned_u, owned_i = user_slot.shape[0] // wide, item_slot.shape[0] // wide
    used, touched = user_need.shape[1], item_need.shape[1]
    upo, each = used // wide, owned_i // ns
    lanes = -(-(used + touched) // 128) * 128
    stages = zs
    steps = qs

    final = pl.pallas_call(
        functools.partial(kernel, peers, ns, upo, 32),
        out_shape=jax.ShapeDtypeStruct((zs, each, qs, rows, rank), BF16),
        in_specs=[HBM] * 13,
        out_specs=HBM,
        scratch_shapes=[
            pltpu.SMEM(user_need.shape, I32),
            pltpu.SMEM(item_need.shape, I32),
            pltpu.SMEM(user_slot.shape, I32),
            pltpu.SMEM(item_slot.shape, I32),
            pltpu.SMEM((tiles,), I32),
            pltpu.SMEM((tiles,), I32),
            pltpu.SMEM((tiles,), I32),
            pltpu.SMEM((1,), I32),
            pltpu.SMEM((1, lanes), I32),
            pltpu.SMEM((peers, 1, lanes), I32),
            pltpu.SMEM((peers, lanes), I32),
            pltpu.SMEM((owned_i, lanes), I32),
            pltpu.SMEM((1, -(-tiles // 128) * 128), I32),
            pltpu.SMEM((1, 128), I32),
            pltpu.VMEM((tiles,), I32),
            pltpu.VMEM((1, -(-tiles // 128) * 128), I32),
            pltpu.VMEM((1, 128), I32),
            pltpu.VMEM((1, lanes), I32),
            pltpu.VMEM((peers, 1, lanes), I32),
            pltpu.VMEM((peers, lanes), I32),
            pltpu.VMEM((peers, lanes), I32),
            pltpu.VMEM((owned_i, lanes), I32),
            [pltpu.VMEM((owned_u, rows, rank), BF16)] * zs,
            pltpu.VMEM((peers, zs * upo, rows, rank), BF16),
            pltpu.VMEM((peers, zs * upo, rows, rank), BF16),
            pltpu.VMEM((used, side, rank), BF16),
            pltpu.VMEM(word_factor.shape, BF16),
            pltpu.VMEM(month_factor.shape, BF16),
            pltpu.VMEM(word_factor.shape, F32),
            pltpu.VMEM(month_factor.shape, F32),
            pltpu.VMEM((tiles, rank), F32),
            pltpu.VMEM((tiles, side, side), BF16),
            pltpu.VMEM((tiles + 1, side, rank), F32),
            pltpu.VMEM((steps, peers, qs // steps, rows, rank), BF16),
            [pltpu.VMEM((peers, qs // steps, rows, rank), BF16)] * steps,
            pltpu.VMEM((peers + 1, qs, rows, rank), F32),
            pltpu.VMEM((qs, ns, each, rows, rank), BF16),
            DMA((8,)),
            DMA,
            DMA,
            DMA,
            DMA,
            DMA,
            DMA,
            DMA,
            DMA,
            DMA,
            DMA,
            DMA((zs,)),
            DMA((stages,)),
            DMA((stages,)),
            DMA((steps,)),
            DMA((steps,)),
            DMA((2,)),
            DMA((2,)),
        ],
        compiler_params=pltpu.CompilerParams(
            collective_id=0, has_side_effects=True, vmem_limit_bytes=58 << 20
        ),
        name="mttkrp",
    )(
        user_need, item_need, user_slot, item_slot, tile_user, tile_word, tile_month, tile_live,
        tile_item, tile_data, user_factor.reshape(owned_u, qs, rows, rank), word_factor, month_factor,
    )
    return jnp.sum(final.astype(F32), axis=0).reshape(-1, rank)


def solution(mesh):
    return jax.shard_map(
        shards,
        mesh=mesh,
        in_specs=(
            P(("wide", "narrow"), None, None),
            P(("wide", "narrow")),
            P(("wide", "narrow")),
            P(("wide", "narrow")),
            P(("wide", "narrow")),
            P(("wide", "narrow")),
            P(("wide", "narrow"), None),
            P(("wide", "narrow"), None),
            P(),
            P(),
            P("wide", None),
            P(),
            P(),
        ),
        out_specs=P(("wide", "narrow"), None),
        check_vma=False,
    )
```
